32 devices in a mesh: grp: 2 (over y), occ: 4 (over z), aux: 2 (over x), vir: 2 (over core).
Axes of the slice: x: 2, y: 2, z: 4, core: 2. Of those that a mesh axis runs over, the one named last changes fastest.
Arguments:
- integrals: bfloat16 [4, 1024, 8, 1280], P('occ', 'aux', 'grp', 'vir'), parts along dimension 2, may hold values from -0.59765625 to 0.59765625
- occ_energy: float32 [8], P('grp'), parts along dimension 0, may hold values from -1.5 to -0.3
- vir_energy: float32 [2560], P('grp'), parts along dimension 0, may hold values from 0.2 to 3
- round_owner: int32 [4], P('grp'), parts along dimension 0, may hold values from 0 to 3, as said below
Outputs:
- gamma_field: float32 [8, 1024, 4, 1280], P('grp', 'aux', 'occ', 'vir'), parts along dimension 0
The draws below stay inside these ranges and needn't reach their ends.
There are 2 independent parts, one for each index of `grp`. The reference program is written for one: setup_inputs(seed, part) draws one part's arguments, and reference() takes and returns one part's arrays. A program takes and returns all parts, laid end to end along the dimension named above; each array names one. Nothing has to cross between parts.
Inputs may be any that keep to these rules, and one draw needn't show every extreme that they name: `round_owner`: the 2 owners are distinct.
All inputs are finite; a program needn't handle non-finite values.
Results may differ from the reference program's by a relative error of at most 0.0085.
Values may be sent and summed in bfloat16 or wider, within the bound.
No kernel may reach another device: no remote copies, remote signals or barrier semaphores. Data moves between devices by JAX's collectives and lax.ppermute only.
A program may use at most 64 MiB of HBM per device.

```python
import jax
import jax.numpy as jnp
from jax import lax

NAUX = 4096
NVIR = 1280
OCC_DEV = 1
ROUNDS = 2
NOCC = 4
OWNERS = 4
N_OCC = 4
N_AUX = 2


def draw_round_owner(key, part):
    ordering = jax.random.permutation(key, OWNERS)
    return ordering[:ROUNDS].astype(jnp.int32)


def level_of(rng, extent, shards, least, high):
    gain, own = 1.0, jax.random.fold_in(rng, 6)
    for dim, blocks in shards:
        heights = jnp.exp(jax.random.uniform(jax.random.fold_in(own, dim), (blocks,), jnp.float32, least / len(shards), high / len(shards)))
        gain = gain * jnp.repeat(heights, extent[dim] // blocks).reshape([-1 if axis == dim else 1 for axis in range(len(extent))])
    return gain


def normal_values(rng, dims, scale, bound, split=(), held_as=jnp.bfloat16):
    values = scale * jax.random.normal(rng, dims, jnp.float32)
    if split:
        values = values * level_of(rng, dims, split, -0.22, 0.18)
    return jnp.clip(values, -bound, bound).astype(held_as)


def setup_inputs(seed: int = 0, part: int = 0) -> dict:
    keys = jax.random.split(jax.random.key(seed), 5)
    part_keys = jax.random.split(jax.random.fold_in(keys[4], part), 5)
    return {
        "integrals": normal_values(part_keys[0], (N_OCC, NAUX // N_OCC, NOCC, NVIR), 0.1, 0.59765625, ((0, 4), (1, 2), (3, 2))),
        "occ_energy": jnp.clip(jax.random.uniform(part_keys[1], (NOCC,), jnp.float32, -1.5, -0.3), -1.5, -0.3),
        "vir_energy": jnp.clip(jax.random.uniform(part_keys[2], (NVIR,), jnp.float32, 0.2, 3.0), 0.2, 3.0),
        "round_owner": draw_round_owner(jax.random.fold_in(jax.random.fold_in(keys[4], part), 71), part),
    }


def reference(integrals, occ_energy, vir_energy, round_owner):
    group_rows = NAUX // (N_OCC * N_AUX)
    grouped = integrals.reshape(N_OCC, N_AUX, group_rows, NOCC, NVIR).astype(jnp.float32)
    gamma_total = jnp.zeros((NOCC, N_OCC, N_AUX, group_rows, NVIR), jnp.float32)
    for turn_index in range(ROUNDS):
        owner = round_owner[turn_index].astype(jnp.int32)
        owner_block = lax.dynamic_slice_in_dim(grouped, owner * OCC_DEV, OCC_DEV, axis=3)
        energy_j = lax.dynamic_slice_in_dim(occ_energy, owner * OCC_DEV, OCC_DEV)

        def one_orbital(index):
            column = lax.dynamic_slice_in_dim(grouped, index, 1, axis=3)[:, :, :, 0, :]
            partial_value = jnp.einsum("sgra,sgrjb->gjab", column, owner_block, precision=lax.Precision.HIGHEST)
            rounded = lax.optimization_barrier(partial_value.astype(jnp.bfloat16))
            pair = jnp.sum(rounded.astype(jnp.float32), axis=0)
            base = occ_energy[index] + energy_j[:, None] - vir_energy[None, :]
            amplitude = lax.optimization_barrier((pair / (base[:, :, None] - vir_energy[None, None, :])).astype(jnp.bfloat16))
            return jnp.einsum("jab,sgrjb->sgra", amplitude.astype(jnp.float32), owner_block, precision=lax.Precision.HIGHEST)

        gamma_total = gamma_total + lax.map(one_orbital, jnp.arange(NOCC, dtype=jnp.int32))
    return jnp.transpose(gamma_total, (1, 2, 3, 0, 4)).reshape(N_OCC, NAUX // N_OCC, NOCC, NVIR)
```

```python
import jax
import jax.numpy as jnp
from jax import lax
from jax.sharding import PartitionSpec as P

ROUNDS = 2


def exchange_sum(part, axis, n):
    total = part.astype(jnp.float32)
    for d in range(1, n):
        perm = [(k, (k + d) % n) for k in range(n)]
        total = total + lax.ppermute(part, axis, perm).astype(jnp.float32)
    return total


def column_chunks(width):
    if width % 128 or width < 512:
        return [(t, 0, width) for t in range(ROUNDS)]
    big = (width // 256) * 128
    return [(0, 0, big), (0, big, width - big), (1, 0, width - big), (1, width - big, big)]


def regroup_four(x, me):
    slots = [lax.dynamic_index_in_dim(x, me, 1, keepdims=False)]
    for k in (1, 2, 3):
        send = lax.dynamic_index_in_dim(x, me ^ k, 1, keepdims=False)
        slots.append(lax.ppermute(send, "occ", [(z, z ^ k) for z in range(4)]))
    return jnp.concatenate(slots, axis=0)


def gather_four(own, me):
    rows = own.shape[0]
    near = lax.ppermute(own, "occ", [(0, 1), (1, 0), (2, 3), (3, 2)])
    half = jnp.concatenate([own, near], axis=0)
    mid = lax.ppermute(half, "occ", [(1, 2), (2, 1)])
    end = lax.ppermute(mid, "occ", [(1, 0), (2, 3)])
    is_mid = (me == 1) | (me == 2)
    swapped = jnp.concatenate([mid[rows:], mid[:rows]], axis=0)
    far = jnp.where(is_mid, swapped, end)
    return jnp.concatenate([half, far], axis=0)


def local(integrals, occ_energy, vir_energy, round_owner):
    n_occ = lax.axis_size("occ")
    n_aux = lax.axis_size("aux")
    me = lax.axis_index("occ")
    core = lax.axis_index("vir")
    x = integrals[0]
    rows, _, width = x.shape
    four = n_occ == 4
    if four:
        mine = regroup_four(x, me)
    else:
        mine = lax.all_to_all(x, "occ", split_axis=1, concat_axis=0, tiled=True)[:, 0]
    energy_i = lax.dynamic_slice_in_dim(occ_energy, me, 1)
    energy_a = lax.dynamic_slice_in_dim(vir_energy, core * width, width)
    gamma = None
    for turn, start, size in column_chunks(width):
        owner = round_owner[turn]
        own = lax.dynamic_slice(x, (0, owner, start), (rows, 1, size))[:, 0]
        if four:
            whole = gather_four(own, me)
        else:
            whole = lax.all_gather(own, "occ", axis=0, tiled=True)
        other = lax.ppermute(whole, "vir", [(0, 1), (1, 0)])
        partial_value = jnp.concatenate(
            [
                jnp.einsum("pb,pa->ba", block, mine, preferred_element_type=jnp.float32).astype(jnp.bfloat16)
                for block in (whole, other)
            ],
            axis=0,
        )
        pair = exchange_sum(partial_value, "aux", n_aux)
        energy_j = lax.dynamic_slice_in_dim(occ_energy, owner, 1)
        energy_b = jnp.concatenate(
            [
                lax.dynamic_slice_in_dim(vir_energy, half * width + start, size)
                for half in (core, 1 - core)
            ]
        )
        base = energy_i + energy_j - energy_a
        amplitude = (pair / (base[None, :] - energy_b[:, None])).astype(jnp.bfloat16)
        for k, block in enumerate((whole, other)):
            term = jnp.dot(block, amplitude[k * size : (k + 1) * size], preferred_element_type=jnp.float32)
            gamma = term if gamma is None else gamma + term
    gamma = gamma.reshape(n_occ, rows, width)
    if four:
        gamma = jnp.stack([lax.dynamic_index_in_dim(gamma, s ^ me, 0, keepdims=False) for s in range(4)])
    return gamma[:, :, None, :]


def solution(mesh):
    placed = (P("occ", "aux", "grp", "vir"), P("grp"), P("grp"), P("grp"))
    return jax.shard_map(
        local, mesh=mesh, in_specs=placed, out_specs=P("grp", "aux", "occ", "vir"), check_vma=False
    )
```

```python
import functools

import jax
import jax.numpy as jnp
from jax import lax
from jax.experimental import pallas as pl
from jax.experimental.pallas import tpu as pltpu
from jax.sharding import PartitionSpec as P

ROUNDS = 2
LANES = 128
SWAP = [(0, 1), (1, 0)]
PAIRS = [(0, 1), (1, 0), (2, 3), (3, 2)]
SKIPS = [(0, 2), (2, 0), (1, 3), (3, 1)]
MIDDLE = [(1, 2), (2, 1)]
ENDS = [(0, 3), (3, 0)]
OUTWARD = [(1, 0), (2, 3)]
F32 = jnp.float32
BF16 = jnp.bfloat16


def column_chunks(width):
    cut = (width // (2 * LANES)) * LANES
    if width % LANES or not cut:
        return [(t, 0, width) for t in range(ROUNDS)]
    return [(0, 0, cut), (0, cut, width - cut), (1, 0, width - cut), (1, width - cut, cut)]


def pair_kernel(near_ref, far_ref, mine_ref, out_ref, acc_ref):
    k = pl.program_id(0)

    @pl.when(k == 0)
    def _():
        acc_ref[...] = jnp.zeros_like(acc_ref)

    def add(ref):
        acc_ref[...] += lax.dot_general(
            ref[...], mine_ref[...], (((0,), (0,)), ((), ())), preferred_element_type=F32
        )

    pl.when(k < 2)(lambda: add(near_ref))
    pl.when(k >= 2)(lambda: add(far_ref))

    @pl.when(k == 3)
    def _():
        out_ref[...] = acc_ref[...].astype(BF16)


def pair_sum(near, far, mine):
    rows, size = near.shape[0] // 2, near.shape[1]
    width = mine.shape[1]
    return pl.pallas_call(
        pair_kernel,
        grid=(4,),
        in_specs=[
            pl.BlockSpec((rows, size), lambda k: (jnp.minimum(k, 1), 0)),
            pl.BlockSpec((rows, size), lambda k: (jnp.maximum(k - 2, 0), 0)),
            pl.BlockSpec((rows, width), lambda k: (k, 0)),
        ],
        out_specs=pl.BlockSpec((size, width), lambda k: (0, 0)),
        out_shape=jax.ShapeDtypeStruct((size, width), BF16),
        scratch_shapes=[pltpu.VMEM((size, width), F32)],
        compiler_params=pltpu.CompilerParams(vmem_limit_bytes=24 << 20),
        cost_estimate=pl.CostEstimate(
            flops=8 * rows * size * width,
            bytes_accessed=8 * rows * (size + width) + 2 * size * width,
            transcendentals=0,
        ),
    )(near, far, mine)


def gamma_kernel(n_aux, last, order_ref, *refs):
    del order_ref
    n_in = 2 * (n_aux + 3) + 1 + (0 if last == "first" else 1)
    ins, out_ref, amp_ref = refs[:n_in], refs[n_in], refs[n_in + 1]
    base_ref = ins[0]
    halves = [ins[1 + h * (n_aux + 3) : 1 + (h + 1) * (n_aux + 3)] for h in range(2)]
    r = pl.program_id(0)
    blocks = pl.num_programs(0)

    @pl.when(r == 0)
    def _():
        for h, half in enumerate(halves):
            total = half[0][...].astype(F32)
            for other in half[1:n_aux]:
                total = total + other[...].astype(F32)
            amp_ref[h] = (total / (base_ref[...] - half[n_aux][...])).astype(BF16)

    def run(which):
        value = jnp.dot(halves[0][n_aux + 1 + which][...], amp_ref[0], preferred_element_type=F32)
        value += jnp.dot(halves[1][n_aux + 1 + which][...], amp_ref[1], preferred_element_type=F32)
        if last != "first":
            value += ins[-1][...]
        if last == "last":
            height, width = value.shape
            step = width // LANES
            for c in range(step):
                out_ref[pl.ds(c, height, stride=step), :] = value[:, c * LANES : (c + 1) * LANES]
        else:
            out_ref[...] = value

    pl.when(r < blocks // 2)(lambda: run(0))
    pl.when(r >= blocks // 2)(lambda: run(1))


def gamma_step(order, base, halves, acc, last):
    n_aux = len(halves[0]) - 3
    near = halves[0][-2]
    rows, size = near.shape[0] // 2, near.shape[1]
    width = base.shape[1]
    block = rows // 2
    full = lambda shape: pl.BlockSpec(shape, lambda r, order: (0, 0))
    specs, args = [full((1, width))], [base]
    for half in halves:
        specs += [full((size, width))] * n_aux + [full((size, 1))]
        specs += [
            pl.BlockSpec((block, size), lambda r, order: (jnp.minimum(r, 3), 0)),
            pl.BlockSpec((block, size), lambda r, order: (jnp.maximum(r - 4, 0), 0)),
        ]
        args += list(half)
    if acc is not None:
        specs.append(pl.BlockSpec((block, width), lambda r, order: (r, 0)))
        args.append(acc)
    if last:
        step = width // LANES
        out_shape = jax.ShapeDtypeStruct((4 * rows * step, LANES), F32)
        out_spec = pl.BlockSpec((block * step, LANES), lambda r, order: (order[r // 2] * 2 + r % 2, 0))
    else:
        out_shape = jax.ShapeDtypeStruct((4 * rows, width), F32)
        out_spec = pl.BlockSpec((block, width), lambda r, order: (r, 0))
    mode = "last" if last else ("first" if acc is None else "more")
    return pl.pallas_call(
        functools.partial(gamma_kernel, n_aux, mode),
        grid_spec=pltpu.PrefetchScalarGridSpec(
            num_scalar_prefetch=1,
            grid=(8,),
            in_specs=specs,
            out_specs=out_spec,
            scratch_shapes=[pltpu.VMEM((2, size, width), BF16)],
        ),
        out_shape=out_shape,
        compiler_params=pltpu.CompilerParams(vmem_limit_bytes=32 << 20),
        cost_estimate=pl.CostEstimate(
            flops=16 * rows * size * width,
            bytes_accessed=16 * rows * size + 4 * n_aux * size * width + 32 * rows * width,
            transcendentals=0,
        ),
    )(order, *args)


def shifted(part, axis, n):
    return [part] + [lax.ppermute(part, axis, [(k, (k + d) % n) for k in range(n)]) for d in range(1, n)]


def local_four(integrals, occ_energy, vir_energy, round_owner):
    n_aux = lax.axis_size("aux")
    me = lax.axis_index("occ")
    core = lax.axis_index("vir")
    by_orbital = lax.optimization_barrier(jnp.transpose(integrals[0], (1, 0, 2)))
    rows, width = by_orbital.shape[1:]
    is_mid = (me == 1) | (me == 2)
    orbital = lambda k: lax.dynamic_index_in_dim(by_orbital, k, 0, keepdims=False)

    b1 = lax.ppermute(orbital(me ^ 1), "occ", PAIRS)
    across = orbital(me ^ 3)
    b3_mid = lax.ppermute(across, "occ", MIDDLE)
    b2 = lax.ppermute(orbital(me ^ 2), "occ", SKIPS)
    own = [orbital(round_owner[t]) for t in range(ROUNDS)]
    near = [lax.ppermute(own[0], "occ", PAIRS)]
    b3_end = lax.ppermute(across, "occ", ENDS)
    near.append(lax.ppermute(own[1], "occ", PAIRS))
    mine = jnp.concatenate([orbital(me), b1, b2, jnp.where(is_mid, b3_mid, b3_end)], axis=0)

    energy_i = lax.dynamic_slice_in_dim(occ_energy, me, 1)
    energy_a = lax.dynamic_slice_in_dim(vir_energy, core * width, width)
    order = (jnp.arange(4, dtype=jnp.int32)) ^ me.astype(jnp.int32)
    chunks = column_chunks(width)
    acc = None
    for index, (turn, start, size) in enumerate(chunks):
        columns = slice(start, start + size)
        half = jnp.concatenate([own[turn][:, columns], near[turn][:, columns]], axis=0)
        half_swap = lax.ppermute(half, "vir", SWAP)
        mid = lax.ppermute(half, "occ", MIDDLE)
        end = lax.ppermute(mid, "occ", OUTWARD)
        turned = jnp.concatenate([mid[rows:], mid[:rows]], axis=0)
        far = jnp.where(is_mid, turned, end)
        far_swap = lax.ppermute(far, "vir", SWAP)
        energy_j = lax.dynamic_slice_in_dim(occ_energy, round_owner[turn], 1)
        base = (energy_i + energy_j - energy_a)[None, :]
        halves = []
        for which, blocks in ((core, (half, far)), (1 - core, (half_swap, far_swap))):
            energy_b = lax.dynamic_slice_in_dim(vir_energy, which * width + start, size)[:, None]
            part = pair_sum(*blocks, mine)
            halves.append((*shifted(part, "aux", n_aux), energy_b, *blocks))
        acc = gamma_step(order, base, halves, acc, index == len(chunks) - 1)
    return acc.reshape(4, rows, 1, width)


def local_any(integrals, occ_energy, vir_energy, round_owner):
    n_aux = lax.axis_size("aux")
    me = lax.axis_index("occ")
    core = lax.axis_index("vir")
    x = integrals[0]
    rows, n_occ, width = x.shape
    mine = lax.all_to_all(x, "occ", split_axis=1, concat_axis=0, tiled=True)[:, 0]
    energy_i = lax.dynamic_slice_in_dim(occ_energy, me, 1)
    energy_a = lax.dynamic_slice_in_dim(vir_energy, core * width, width)
    gamma = jnp.zeros(mine.shape, F32)
    for turn in range(ROUNDS):
        owner = round_owner[turn]
        own = lax.dynamic_index_in_dim(x, owner, 1, keepdims=False)
        whole = lax.all_gather(own, "occ", axis=0, tiled=True)
        other = lax.ppermute(whole, "vir", SWAP)
        energy_j = lax.dynamic_slice_in_dim(occ_energy, owner, 1)
        base = (energy_i + energy_j - energy_a)[None, :]
        for which, block in ((core, whole), (1 - core, other)):
            energy_b = lax.dynamic_slice_in_dim(vir_energy, which * width, width)[:, None]
            part = jnp.einsum("pb,pa->ba", block, mine, preferred_element_type=F32).astype(BF16)
            pair = sum(p.astype(F32) for p in shifted(part, "aux", n_aux))
            amplitude = (pair / (base - energy_b)).astype(BF16)
            gamma = gamma + jnp.dot(block, amplitude, preferred_element_type=F32)
    return gamma.reshape(-1, rows, 1, width)


def solution(mesh):
    placed = (P("occ", "aux", "grp", "vir"), P("grp"), P("grp"), P("grp"))
    local = local_four if mesh.shape["occ"] == 4 else local_any
    return jax.shard_map(
        local, mesh=mesh, in_specs=placed, out_specs=P("grp", "aux", "occ", "vir"), check_vma=False
    )
```

```python
import functools

import jax
import jax.numpy as jnp
from jax import lax
from jax.experimental import pallas as pl
from jax.experimental.pallas import tpu as pltpu
from jax.sharding import PartitionSpec as P

ROUNDS = 2
LANES = 128
SWAP = [(0, 1), (1, 0)]
PAIRS = [(0, 1), (1, 0), (2, 3), (3, 2)]
SKIPS = [(0, 2), (2, 0), (1, 3), (3, 1)]
MIDDLE = [(1, 2), (2, 1)]
ENDS = [(0, 3), (3, 0)]
OUTWARD = [(1, 0), (2, 3)]
F32 = jnp.float32
BF16 = jnp.bfloat16


def column_chunks(width):
    cut = (width // (2 * LANES)) * LANES
    if width % LANES or not cut:
        return [(t, 0, width) for t in range(ROUNDS)]
    return [(0, 0, cut), (0, cut, width - cut), (1, 0, width - cut), (1, width - cut, cut)]


def after(value, *done):
    return lax.optimization_barrier((value, *done))[0]


def pair_kernel(half_index, par_ref, near_ref, far_ref, *refs):
    del par_ref
    slots, out_ref, acc_ref = refs[:4], refs[-2], refs[-1]
    k = pl.program_id(0)

    for step in range(4):

        @pl.when(k == step)
        def _(step=step):
            value = lax.dot_general(
                (near_ref if step < 2 else far_ref)[...],
                slots[step][...],
                (((0,), (0,)), ((), ())),
                preferred_element_type=F32,
            )
            if step:
                value += acc_ref[...]
            if step < 3:
                acc_ref[...] = value
            else:
                out_ref[...] = value.astype(BF16)


def pair_sum(par, near, far, mine, into):
    rows, size = near.shape[0] // 2, near.shape[1]
    width = mine[0][0].shape[1]
    half_index = 0 if into is None else 1
    specs = [
        pl.BlockSpec((rows, size), lambda k, par: (jnp.minimum(k, 1) ^ par[0], 0)),
        pl.BlockSpec((rows, size), lambda k, par: (jnp.maximum(k - 2, 0) ^ par[0], 0)),
        *[pl.BlockSpec((rows, width), lambda k, par, at=at: (at, 0)) for _, at in mine],
    ]
    args = [near, far, *[array for array, _ in mine]]
    if half_index:
        specs.append(pl.BlockSpec(memory_space=pl.ANY))
        args.append(into)
    return pl.pallas_call(
        functools.partial(pair_kernel, half_index),
        grid_spec=pltpu.PrefetchScalarGridSpec(
            num_scalar_prefetch=1,
            grid=(4,),
            in_specs=specs,
            out_specs=pl.BlockSpec((size, width), lambda k, par: (half_index, 0)),
            scratch_shapes=[pltpu.VMEM((size, width), F32)],
        ),
        out_shape=jax.ShapeDtypeStruct((2 * size, width), BF16),
        input_output_aliases={len(args): 0} if half_index else {},
        compiler_params=pltpu.CompilerParams(vmem_limit_bytes=24 << 20),
        cost_estimate=pl.CostEstimate(
            flops=8 * rows * size * width,
            bytes_accessed=8 * rows * (size + width) + 2 * size * width,
            transcendentals=0,
        ),
    )(par, *args)


def gamma_kernel(n_aux, turn, start, mode, order_ref, core_ref, base_ref, column_ref, *refs):
    del order_ref
    parts, blocks = refs[:n_aux], refs[n_aux : n_aux + 4]
    refs = refs[n_aux + 4 :]
    if mode != "first":
        acc_ref, refs = refs[0], refs[1:]
    out_ref, amp_ref = refs
    size, width = amp_ref.shape[1:]
    r = pl.program_id(0)
    count = pl.num_programs(0)

    @pl.when(r == 0)
    def _():
        for h in range(2):
            lines = slice(h * size, (h + 1) * size)
            total = parts[0][lines, :].astype(F32)
            for other in parts[1:]:
                total = total + other[lines, :].astype(F32)
            which = core_ref[0] if h == 0 else 1 - core_ref[0]
            first = pl.multiple_of(which * width + start, LANES)
            below = base_ref[turn : turn + 1, :] - column_ref[pl.ds(first, size), :]
            amp_ref[h] = (total / below).astype(BF16)

    def run(which):
        value = jnp.dot(blocks[which][...], amp_ref[0], preferred_element_type=F32)
        value += jnp.dot(blocks[2 + which][...], amp_ref[1], preferred_element_type=F32)
        if mode != "first":
            value += acc_ref[...]
        if mode == "last":
            height = value.shape[0]
            step = width // LANES
            for c in range(step):
                out_ref[pl.ds(c, height, stride=step), :] = value[:, c * LANES : (c + 1) * LANES]
        else:
            out_ref[...] = value

    pl.when(r < count // 2)(lambda: run(0))
    pl.when(r >= count // 2)(lambda: run(1))


def gamma_step(table, turn, start, parts, blocks, acc, last):
    order, core, base, column = table
    near = blocks[0]
    rows, size = near.shape[0] // 2, near.shape[1]
    width = base.shape[1]
    block = rows // 2
    full = lambda array: pl.BlockSpec(array.shape, lambda r, order, core: (0, 0))
    args = [base, column, *parts]
    specs = [full(array) for array in args]
    for _ in range(2):
        specs += [
            pl.BlockSpec((block, size), lambda r, order, core: (jnp.minimum(r, 3), 0)),
            pl.BlockSpec((block, size), lambda r, order, core: (jnp.maximum(r - 4, 0), 0)),
        ]
    args += blocks
    if acc is not None:
        specs.append(pl.BlockSpec((block, width), lambda r, order, core: (r, 0)))
        args.append(acc)
    if last:
        step = width // LANES
        out_shape = jax.ShapeDtypeStruct((4 * rows * step, LANES), F32)
        out_spec = pl.BlockSpec(
            (block * step, LANES), lambda r, order, core: (order[r // 2] * 2 + r % 2, 0)
        )
    else:
        out_shape = jax.ShapeDtypeStruct((4 * rows, width), F32)
        out_spec = pl.BlockSpec((block, width), lambda r, order, core: (r, 0))
    mode = "last" if last else ("first" if acc is None else "more")
    return pl.pallas_call(
        functools.partial(gamma_kernel, len(parts), turn, start, mode),
        grid_spec=pltpu.PrefetchScalarGridSpec(
            num_scalar_prefetch=2,
            grid=(8,),
            in_specs=specs,
            out_specs=out_spec,
            scratch_shapes=[pltpu.VMEM((2, size, width), BF16)],
        ),
        out_shape=out_shape,
        compiler_params=pltpu.CompilerParams(vmem_limit_bytes=32 << 20),
        cost_estimate=pl.CostEstimate(
            flops=16 * rows * size * width,
            bytes_accessed=16 * rows * size + 4 * len(parts) * size * width + 32 * rows * width,
            transcendentals=0,
        ),
    )(order, core, *args)


def shifted(part, axis, n):
    return [part] + [lax.ppermute(part, axis, [(k, (k + d) % n) for k in range(n)]) for d in range(1, n)]


def local_four(integrals, occ_energy, vir_energy, round_owner):
    n_aux = lax.axis_size("aux")
    me = lax.axis_index("occ").astype(jnp.int32)
    core = lax.axis_index("vir").astype(jnp.int32)
    by_orbital = lax.optimization_barrier(jnp.transpose(integrals[0], (1, 0, 2)))
    rows, width = by_orbital.shape[1:]
    is_mid = (me == 1) | (me == 2)
    odd = me % 2
    orbital = lambda k: lax.dynamic_index_in_dim(by_orbital, k, 0, keepdims=False)

    own = [orbital(round_owner[t]) for t in range(ROUNDS)]
    across = orbital(me ^ 3)
    beside = lax.ppermute(jnp.concatenate([own[0], orbital(me ^ 1)], axis=0), "occ", PAIRS)
    b3_mid = lax.ppermute(across, "occ", MIDDLE)
    b2 = lax.ppermute(orbital(me ^ 2), "occ", SKIPS)
    b3_end = lax.ppermute(across, "occ", ENDS)
    near = [beside[:rows], lax.ppermute(own[1], "occ", PAIRS)]
    mine = [(orbital(me), 0), (beside, 1), (b2, 0), (jnp.where(is_mid, b3_mid, b3_end), 0)]

    energy_i = lax.dynamic_slice_in_dim(occ_energy, me, 1)
    energy_a = lax.dynamic_slice_in_dim(vir_energy, core * width, width)
    energy_j = jnp.take(occ_energy, round_owner)
    base = energy_i + energy_j[:, None] - energy_a[None, :]
    order = jnp.arange(4, dtype=jnp.int32) ^ (me & 2)
    table = (order, core[None], base, vir_energy[:, None])

    chunks = column_chunks(width)
    count = len(chunks)
    half, mid, part = [None] * count, [None] * count, [None] * count

    def hop(c, *done):
        turn, start, size = chunks[c]
        columns = slice(start, start + size)
        pieces = own[turn][:, columns], near[turn][:, columns]
        half[c] = jnp.where(odd == 1, jnp.concatenate(pieces[::-1], axis=0), jnp.concatenate(pieces, axis=0))
        if done:
            half[c] = after(half[c], *done)
        mid[c] = lax.ppermute(half[c], "occ", MIDDLE)

    hop(0, b3_mid)
    hop(1, b2, b3_end)
    acc, total = None, []
    for c, (turn, start, size) in enumerate(chunks):
        if c + 2 < count:
            hop(c + 2, mid[c], *([part[c - 1]] if c else []))
        half_swap = lax.ppermute(half[c], "vir", SWAP)
        end = lax.ppermute(mid[c], "occ", OUTWARD)
        if c + 1 < count:
            end = after(end, mid[c + 1])
        far = jnp.where(is_mid, mid[c], end)
        far_swap = lax.ppermute(far, "vir", SWAP)
        if c == 0:
            far = after(far, near[1])
        if c > 1:
            far = after(far, total[c - 2])
        for blocks in ((half[c], far), (half_swap, far_swap)):
            part[c] = pair_sum(odd[None], *blocks, mine, part[c])
        parts = shifted(part[c], "aux", n_aux)
        acc = gamma_step(table, turn, start, parts, [half[c], far, half_swap, far_swap], acc, c == count - 1)
        total.append(acc)
    return acc.reshape(4, rows, 1, width)


def local_any(integrals, occ_energy, vir_energy, round_owner):
    n_aux = lax.axis_size("aux")
    me = lax.axis_index("occ")
    core = lax.axis_index("vir")
    x = integrals[0]
    rows, n_occ, width = x.shape
    mine = lax.all_to_all(x, "occ", split_axis=1, concat_axis=0, tiled=True)[:, 0]
    energy_i = lax.dynamic_slice_in_dim(occ_energy, me, 1)
    energy_a = lax.dynamic_slice_in_dim(vir_energy, core * width, width)
    gamma = jnp.zeros(mine.shape, F32)
    for turn in range(ROUNDS):
        owner = round_owner[turn]
        own = lax.dynamic_index_in_dim(x, owner, 1, keepdims=False)
        whole = lax.all_gather(own, "occ", axis=0, tiled=True)
        other = lax.ppermute(whole, "vir", SWAP)
        energy_j = lax.dynamic_slice_in_dim(occ_energy, owner, 1)
        base = (energy_i + energy_j - energy_a)[None, :]
        for which, block in ((core, whole), (1 - core, other)):
            energy_b = lax.dynamic_slice_in_dim(vir_energy, which * width, width)[:, None]
            part = jnp.einsum("pb,pa->ba", block, mine, preferred_element_type=F32).astype(BF16)
            pair = sum(p.astype(F32) for p in shifted(part, "aux", n_aux))
            amplitude = (pair / (base - energy_b)).astype(BF16)
            gamma = gamma + jnp.dot(block, amplitude, preferred_element_type=F32)
    return gamma.reshape(-1, rows, 1, width)


def solution(mesh):
    placed = (P("occ", "aux", "grp", "vir"), P("grp"), P("grp"), P("grp"))
    local = local_four if mesh.shape["occ"] == 4 else local_any
    return jax.shard_map(
        local, mesh=mesh, in_specs=placed, out_specs=P("grp", "aux", "occ", "vir"), check_vma=False
    )
```

```python
import functools

import jax
import jax.numpy as jnp
from jax import lax
from jax.experimental import pallas as pl
from jax.experimental.pallas import tpu as pltpu
from jax.sharding import PartitionSpec as P

ROUNDS = 2
F32 = jnp.float32
BF16 = jnp.bfloat16
LANES = 128
NARROW = 1
SEND = BF16
SWAP = [(0, 1), (1, 0)]
PAIRS = [(0, 1), (1, 0), (2, 3), (3, 2)]
SKIPS = [(0, 2), (2, 0), (1, 3), (3, 1)]
MIDDLE = [(1, 2), (2, 1)]
ENDS = [(0, 3), (3, 0)]
OUTWARD = [(1, 0), (2, 3)]


def column_chunks(width):
    cut = (width // (2 * LANES)) * LANES
    if width % LANES or not cut:
        return [(t, 0, width) for t in range(ROUNDS)]
    return [(0, 0, cut), (0, cut, width - cut), (1, 0, width - cut), (1, width - cut, cut)]


def after(value, *done):
    return lax.optimization_barrier((value, *done))[0]


def pack_kernel(chunk_starts, index_ref, first_ref, second_ref, *outs):
    k = pl.program_id(0)

    def put(ref):
        for start, out_ref in zip(chunk_starts, outs):
            out_ref[...] = ref[:, start : start + out_ref.shape[1]]

    pl.when(k == 0)(lambda: put(first_ref))
    pl.when(k == 1)(lambda: put(second_ref))


def pack(index, first, second, pieces):
    second, at = second
    rows, width = first.shape
    return pl.pallas_call(
        functools.partial(pack_kernel, [start for start, _ in pieces]),
        grid_spec=pltpu.PrefetchScalarGridSpec(
            num_scalar_prefetch=1,
            grid=(2,),
            in_specs=[
                pl.BlockSpec((rows, width), lambda k, index: (0, 0)),
                pl.BlockSpec((rows, width), lambda k, index: (at, 0)),
            ],
            out_specs=[pl.BlockSpec((rows, size), lambda k, index: (k ^ index[0], 0)) for _, size in pieces],
        ),
        out_shape=[jax.ShapeDtypeStruct((2 * rows, size), first.dtype) for _, size in pieces],
        compiler_params=pltpu.CompilerParams(vmem_limit_bytes=16 << 20),
        cost_estimate=pl.CostEstimate(flops=0, bytes_accessed=8 * rows * width, transcendentals=0),
    )(index, first, second)


def pair_kernel(par_ref, near_ref, far_ref, *refs):
    del par_ref
    slots, out_ref, acc_ref = refs[:-2], refs[-2], refs[-1]
    size = near_ref.shape[1]
    k = pl.program_id(0)

    def add(block_ref, which, first, final):
        block = block_ref[...]
        for h in range(len(slots) // 2):
            lines = slice(h * size, (h + 1) * size)
            value = lax.dot_general(
                block, slots[2 * h + which][...], (((0,), (0,)), ((), ())), preferred_element_type=F32
            )
            if not first:
                value += acc_ref[lines, :]
            if final:
                out_ref[lines, :] = value.astype(BF16)
            else:
                acc_ref[lines, :] = value

    pl.when(k == 0)(lambda: add(near_ref, 0, True, False))
    pl.when(k == 1)(lambda: add(near_ref, 0, False, False))
    pl.when(k == 2)(lambda: add(far_ref, 1, False, False))
    pl.when(k == 3)(lambda: add(far_ref, 1, False, True))


def pair_sum(par, near, far, slots):
    rows, size = near.shape[0] // 2, near.shape[1]
    width = slots[0].shape[1]
    lines = len(slots) // 2 * size
    first = lambda k, par: (jnp.minimum(k, 1), 0)
    second = lambda k, par: (jnp.maximum(k - 2, 0), 0)
    return pl.pallas_call(
        pair_kernel,
        grid_spec=pltpu.PrefetchScalarGridSpec(
            num_scalar_prefetch=1,
            grid=(4,),
            in_specs=[
                pl.BlockSpec((rows, size), lambda k, par: (jnp.minimum(k, 1) ^ par[0], 0)),
                pl.BlockSpec((rows, size), lambda k, par: (jnp.maximum(k - 2, 0) ^ par[0], 0)),
                *[pl.BlockSpec((rows, width), first), pl.BlockSpec((rows, width), second)] * (len(slots) // 2),
            ],
            out_specs=pl.BlockSpec((lines, width), lambda k, par: (0, 0)),
            scratch_shapes=[pltpu.VMEM((lines, width), F32)],
        ),
        out_shape=jax.ShapeDtypeStruct((lines, width), BF16),
        compiler_params=pltpu.CompilerParams(vmem_limit_bytes=24 << 20),
        cost_estimate=pl.CostEstimate(
            flops=8 * rows * lines * width,
            bytes_accessed=8 * rows * size + 4 * rows * len(slots) * width + 2 * lines * width,
            transcendentals=0,
        ),
    )(par, near, far, *slots)


def gamma_kernel(n_aux, turn, start, wide, n_add, final, order_ref, core_ref, base_ref, column_ref, *refs):
    del order_ref
    n_blocks = 2 if wide else 4
    parts, refs = refs[:n_aux], refs[n_aux:]
    blocks, refs = refs[:n_blocks], refs[n_blocks:]
    adds, outs, amp_ref = refs[:n_add], refs[n_add:-1], refs[-1]
    size, width = amp_ref.shape[1:]
    r = pl.program_id(0)
    count = pl.num_programs(0)

    @pl.when(r == 0)
    def _():
        for h in range(2):
            lines = slice(h * size, (h + 1) * size)
            total = parts[0][lines, :].astype(F32)
            for other in parts[1:]:
                total = total + other[lines, :].astype(F32)
            which = 1 - core_ref[0] if h and not wide else core_ref[0]
            row = turn + (ROUNDS if h and wide else 0)
            first = pl.multiple_of(which * width + start, LANES)
            below = base_ref[row : row + 1, :] - column_ref[pl.ds(first, size), :]
            amp_ref[h] = (total / below).astype(BF16)

    def run(which):
        if wide:
            for h in range(2):
                value = jnp.dot(blocks[which][...], amp_ref[h], preferred_element_type=F32)
                if n_add:
                    value += adds[h][...]
                outs[h][...] = value.astype(outs[h].dtype)
            return
        value = jnp.dot(blocks[which][...], amp_ref[0], preferred_element_type=F32)
        value += jnp.dot(blocks[2 + which][...], amp_ref[1], preferred_element_type=F32)
        for extra in adds:
            value += extra[...].astype(F32)
        if final:
            height = value.shape[0]
            step = width // LANES
            for c in range(step):
                outs[0][pl.ds(c, height, stride=step), :] = value[:, c * LANES : (c + 1) * LANES]
        else:
            outs[0][...] = value

    pl.when(r < count // 2)(lambda: run(0))
    pl.when(r >= count // 2)(lambda: run(1))


def gamma_step(table, turn, start, parts, blocks, adds, kinds, final=False):
    order, core, base, column = table
    wide = len(blocks) == 2
    rows, size = blocks[0].shape[0] // 2, blocks[0].shape[1]
    width = base.shape[1]
    block = rows // 2
    full = lambda array: pl.BlockSpec(array.shape, lambda r, order, core: (0, 0))
    row_block = pl.BlockSpec((block, width), lambda r, order, core: (r, 0))
    args = [base, column, *parts]
    specs = [full(array) for array in args]
    for _ in range(len(blocks) // 2):
        specs += [
            pl.BlockSpec((block, size), lambda r, order, core: (jnp.minimum(r, 3), 0)),
            pl.BlockSpec((block, size), lambda r, order, core: (jnp.maximum(r - 4, 0), 0)),
        ]
    args += [*blocks, *adds]
    specs += [row_block] * len(adds)
    if final:
        step = width // LANES
        out_shape = [jax.ShapeDtypeStruct((4 * rows * step, LANES), F32)]
        out_specs = [
            pl.BlockSpec((block * step, LANES), lambda r, order, core: (order[r // 2] * 2 + r % 2, 0))
        ]
    else:
        out_shape = [jax.ShapeDtypeStruct((4 * rows, width), kind) for kind in kinds]
        out_specs = [row_block] * len(kinds)
    return pl.pallas_call(
        functools.partial(gamma_kernel, len(parts), turn, start, wide, len(adds), final),
        grid_spec=pltpu.PrefetchScalarGridSpec(
            num_scalar_prefetch=2,
            grid=(8,),
            in_specs=specs,
            out_specs=out_specs,
            scratch_shapes=[pltpu.VMEM((2, size, width), BF16)],
        ),
        out_shape=out_shape,
        compiler_params=pltpu.CompilerParams(vmem_limit_bytes=32 << 20),
        cost_estimate=pl.CostEstimate(
            flops=16 * rows * size * width,
            bytes_accessed=16 * rows * size + 4 * len(parts) * size * width + 32 * rows * width,
            transcendentals=0,
        ),
    )(order, core, *args)


def shifted(part, axis, n):
    return [part] + [lax.ppermute(part, axis, [(k, (k + d) % n) for k in range(n)]) for d in range(1, n)]


def local_four(integrals, occ_energy, vir_energy, round_owner):
    n_aux = lax.axis_size("aux")
    me = lax.axis_index("occ").astype(jnp.int32)
    core = lax.axis_index("vir").astype(jnp.int32)
    by_orbital = lax.optimization_barrier(jnp.transpose(integrals[0], (1, 0, 2)))
    rows, width = by_orbital.shape[1:]
    is_mid = (me == 1) | (me == 2)
    odd = me % 2
    orbital = lambda k: lax.dynamic_index_in_dim(by_orbital, k, 0, keepdims=False)

    own = [orbital(round_owner[t]) for t in range(ROUNDS)]
    across = orbital(me ^ 3)
    beside = lax.ppermute(jnp.concatenate([own[0], orbital(me ^ 1)], axis=0), "occ", PAIRS)
    b3_mid = lax.ppermute(across, "occ", MIDDLE)
    b2 = lax.ppermute(orbital(me ^ 2), "occ", SKIPS)
    b3_end = lax.ppermute(across, "occ", ENDS)
    near = [(beside, 0), (lax.ppermute(own[1], "occ", PAIRS), 0)]

    energy_i = lax.dynamic_slice_in_dim(occ_energy, me, 1)
    energy_j = jnp.take(occ_energy, round_owner)
    bases = [
        energy_i + energy_j[:, None] - lax.dynamic_slice_in_dim(vir_energy, k * width, width)[None, :]
        for k in (core, 1 - core)
    ]
    order = jnp.arange(4, dtype=jnp.int32) ^ (me & 2)
    table = (order, core[None], jnp.concatenate(bases, axis=0), vir_energy[:, None])

    chunks = column_chunks(width)
    count = len(chunks)
    wide = count - NARROW
    half, mid, part, got, total = [None] * count, [None] * count, [None] * count, [None] * count, []

    for t in range(ROUNDS):
        members = [c for c in range(count) if chunks[c][0] == t]
        packed = pack(odd[None], own[t], near[t], [chunks[c][1:] for c in members])
        for c, array in zip(members, packed):
            half[c] = array

    def hop(c, *done):
        mid[c] = lax.ppermute(after(half[c], *done), "occ", MIDDLE)

    hop(0, b3_mid)
    hop(1, b2, b3_end)
    none = jnp.zeros((1,), jnp.int32)
    (mine_near,) = pack(none, orbital(me), (beside, 1), [(0, width)])
    (mine_far,) = pack(none, b2, (jnp.where(is_mid, b3_mid, b3_end), 0), [(0, width)])
    mine_far = after(mine_far, mid[0], near[1][0])
    mine_near_swap = lax.ppermute(mine_near, "vir", SWAP)
    mine_far_swap = lax.ppermute(mine_far, "vir", SWAP)
    pending = []

    def settle(acc, there, *done):
        c, turn, start, parts, blocks = pending.pop(0)
        parts = [after(parts[0], *done), *parts[1:]] if done else parts
        if c >= wide:
            last = c == count - 1
            adds = [*acc, there] if last else acc
            return gamma_step(table, turn, start, parts, blocks, adds, (F32,), final=last), there
        kinds = (F32, F32 if c < wide - 1 else SEND)
        acc = gamma_step(table, turn, start, parts, blocks, acc, kinds)
        if c == wide - 1:
            there = lax.ppermute(acc[1], "vir", SWAP)
            acc = acc[:1]
        return acc, there

    acc, there = (), None
    for c, (turn, start, size) in enumerate(chunks):
        if c + 2 < count:
            hop(c + 2, mid[c], mine_near_swap, *([mine_far_swap] if c else []))
        end = lax.ppermute(mid[c], "occ", OUTWARD)
        if c + 1 < count:
            end = after(end, mid[c + 1])
        here = mid[c]
        if c == 0:
            here = after(here, near[1][0], mine_near_swap, mine_far_swap)
        if c > 1:
            here = after(here, *total[c - 2])
        if c:
            here = after(here, part[c - 1])
        far = jnp.where(is_mid, here, end)
        blocks = [half[c], far]
        if c < wide:
            part[c] = pair_sum(odd[None], *blocks, [mine_near, mine_far, mine_near_swap, mine_far_swap])
        else:
            blocks += [lax.ppermute(half[c], "vir", SWAP), lax.ppermute(far, "vir", SWAP)]
            part[c] = jnp.concatenate(
                [pair_sum(odd[None], *blocks[2 * h : 2 * h + 2], [mine_near, mine_far]) for h in range(2)], axis=0
            )
        got[c] = shifted(part[c], "aux", n_aux)
        pending.append((c, turn, start, got[c], blocks))
        if c:
            acc, there = settle(acc, there, part[c])
            total.append(acc)
    acc, there = settle(acc, there)
    return acc[0].reshape(4, rows, 1, width)


def local_any(integrals, occ_energy, vir_energy, round_owner):
    n_aux = lax.axis_size("aux")
    me = lax.axis_index("occ")
    core = lax.axis_index("vir")
    x = integrals[0]
    rows, n_occ, width = x.shape
    mine = lax.all_to_all(x, "occ", split_axis=1, concat_axis=0, tiled=True)[:, 0]
    energy_i = lax.dynamic_slice_in_dim(occ_energy, me, 1)
    energy_a = lax.dynamic_slice_in_dim(vir_energy, core * width, width)
    gamma = jnp.zeros(mine.shape, F32)
    for turn in range(ROUNDS):
        owner = round_owner[turn]
        own = lax.dynamic_index_in_dim(x, owner, 1, keepdims=False)
        whole = lax.all_gather(own, "occ", axis=0, tiled=True)
        other = lax.ppermute(whole, "vir", SWAP)
        energy_j = lax.dynamic_slice_in_dim(occ_energy, owner, 1)
        base = (energy_i + energy_j - energy_a)[None, :]
        for which, block in ((core, whole), (1 - core, other)):
            energy_b = lax.dynamic_slice_in_dim(vir_energy, which * width, width)[:, None]
            part = jnp.einsum("pb,pa->ba", block, mine, preferred_element_type=F32).astype(BF16)
            pair = sum(p.astype(F32) for p in shifted(part, "aux", n_aux))
            amplitude = (pair / (base - energy_b)).astype(BF16)
            gamma = gamma + jnp.dot(block, amplitude, preferred_element_type=F32)
    return gamma.reshape(-1, rows, 1, width)


def solution(mesh):
    placed = (P("occ", "aux", "grp", "vir"), P("grp"), P("grp"), P("grp"))
    local = local_four if mesh.shape["occ"] == 4 else local_any
    return jax.shard_map(
        local, mesh=mesh, in_specs=placed, out_specs=P("grp", "aux", "occ", "vir"), check_vma=False
    )
```

```python
import functools

import jax
import jax.numpy as jnp
from jax import lax
from jax.experimental import pallas as pl
from jax.experimental.pallas import tpu as pltpu
from jax.sharding import PartitionSpec as P

ROUNDS = 2
F32 = jnp.float32
BF16 = jnp.bfloat16
LANES = 128
NARROW = 1
SEND = BF16
SWAP = [(0, 1), (1, 0)]
PAIRS = [(0, 1), (1, 0), (2, 3), (3, 2)]
SKIPS = [(0, 2), (2, 0), (1, 3), (3, 1)]
MIDDLE = [(1, 2), (2, 1)]
ENDS = [(0, 3), (3, 0)]
OUTWARD = [(1, 0), (2, 3)]


def column_chunks(width):
    cut = (width // (2 * LANES)) * LANES
    if width % LANES or not cut:
        return [(t, 0, width) for t in range(ROUNDS)]
    return [(0, 0, cut), (0, cut, width - cut), (1, 0, width - cut), (1, width - cut, cut)]


def after(value, *done):
    return lax.optimization_barrier((value, *done))[0]


def pack_kernel(chunk_starts, index_ref, first_ref, second_ref, *outs):
    k = pl.program_id(0)

    def put(ref):
        for start, out_ref in zip(chunk_starts, outs):
            out_ref[...] = ref[:, start : start + out_ref.shape[1]]

    pl.when(k == 0)(lambda: put(first_ref))
    pl.when(k == 1)(lambda: put(second_ref))


def pack(index, first, second, pieces):
    second, at = second
    rows, width = first.shape
    return pl.pallas_call(
        functools.partial(pack_kernel, [start for start, _ in pieces]),
        grid_spec=pltpu.PrefetchScalarGridSpec(
            num_scalar_prefetch=1,
            grid=(2,),
            in_specs=[
                pl.BlockSpec((rows, width), lambda k, index: (0, 0)),
                pl.BlockSpec((rows, width), lambda k, index: (at, 0)),
            ],
            out_specs=[pl.BlockSpec((rows, size), lambda k, index: (k ^ index[0], 0)) for _, size in pieces],
        ),
        out_shape=[jax.ShapeDtypeStruct((2 * rows, size), first.dtype) for _, size in pieces],
        compiler_params=pltpu.CompilerParams(vmem_limit_bytes=16 << 20),
        cost_estimate=pl.CostEstimate(flops=0, bytes_accessed=8 * rows * width, transcendentals=0),
    )(index, first, second)


def pair_kernel(par_ref, near_ref, far_ref, *refs):
    del par_ref
    slots, out_ref, acc_ref = refs[:-2], refs[-2], refs[-1]
    size = near_ref.shape[1]
    k = pl.program_id(0)

    def add(block_ref, which, first, final):
        block = block_ref[...]
        for h in range(len(slots) // 2):
            lines = slice(h * size, (h + 1) * size)
            value = lax.dot_general(
                block, slots[2 * h + which][...], (((0,), (0,)), ((), ())), preferred_element_type=F32
            )
            if not first:
                value += acc_ref[lines, :]
            if final:
                out_ref[lines, :] = value.astype(BF16)
            else:
                acc_ref[lines, :] = value

    pl.when(k == 0)(lambda: add(near_ref, 0, True, False))
    pl.when(k == 1)(lambda: add(near_ref, 0, False, False))
    pl.when(k == 2)(lambda: add(far_ref, 1, False, False))
    pl.when(k == 3)(lambda: add(far_ref, 1, False, True))


def pair_sum(par, near, far, slots):
    rows, size = near.shape[0] // 2, near.shape[1]
    width = slots[0].shape[1]
    lines = len(slots) // 2 * size
    first = lambda k, par: (jnp.minimum(k, 1), 0)
    second = lambda k, par: (jnp.maximum(k - 2, 0), 0)
    return pl.pallas_call(
        pair_kernel,
        grid_spec=pltpu.PrefetchScalarGridSpec(
            num_scalar_prefetch=1,
            grid=(4,),
            in_specs=[
                pl.BlockSpec((rows, size), lambda k, par: (jnp.minimum(k, 1) ^ par[0], 0)),
                pl.BlockSpec((rows, size), lambda k, par: (jnp.maximum(k - 2, 0) ^ par[0], 0)),
                *[pl.BlockSpec((rows, width), first), pl.BlockSpec((rows, width), second)] * (len(slots) // 2),
            ],
            out_specs=pl.BlockSpec((lines, width), lambda k, par: (0, 0)),
            scratch_shapes=[pltpu.VMEM((lines, width), F32)],
        ),
        out_shape=jax.ShapeDtypeStruct((lines, width), BF16),
        compiler_params=pltpu.CompilerParams(vmem_limit_bytes=24 << 20),
        cost_estimate=pl.CostEstimate(
            flops=8 * rows * lines * width,
            bytes_accessed=8 * rows * size + 4 * rows * len(slots) * width + 2 * lines * width,
            transcendentals=0,
        ),
    )(par, near, far, *slots)


def gamma_kernel(n_aux, turn, start, wide, n_add, final, order_ref, core_ref, base_ref, column_ref, *refs):
    del order_ref
    n_blocks = 2 if wide else 4
    parts, refs = refs[:n_aux], refs[n_aux:]
    blocks, refs = refs[:n_blocks], refs[n_blocks:]
    adds, outs, amp_ref = refs[:n_add], refs[n_add:-1], refs[-1]
    size, width = amp_ref.shape[1:]
    r = pl.program_id(0)
    count = pl.num_programs(0)

    @pl.when(r == 0)
    def _():
        for h in range(2):
            lines = slice(h * size, (h + 1) * size)
            total = parts[0][lines, :].astype(F32)
            for other in parts[1:]:
                total = total + other[lines, :].astype(F32)
            which = 1 - core_ref[0] if h and not wide else core_ref[0]
            row = turn + (ROUNDS if h and wide else 0)
            first = pl.multiple_of(which * width + start, LANES)
            below = base_ref[row : row + 1, :] - column_ref[pl.ds(first, size), :]
            amp_ref[h] = (total / below).astype(BF16)

    def run(which):
        if wide:
            for h in range(2):
                value = jnp.dot(blocks[which][...], amp_ref[h], preferred_element_type=F32)
                if n_add:
                    value += adds[h][...]
                outs[h][...] = value.astype(outs[h].dtype)
            return
        value = jnp.dot(blocks[which][...], amp_ref[0], preferred_element_type=F32)
        value += jnp.dot(blocks[2 + which][...], amp_ref[1], preferred_element_type=F32)
        for extra in adds:
            value += extra[...].astype(F32)
        if final:
            height = value.shape[0]
            step = width // LANES
            for c in range(step):
                outs[0][pl.ds(c, height, stride=step), :] = value[:, c * LANES : (c + 1) * LANES]
        else:
            outs[0][...] = value

    pl.when(r < count // 2)(lambda: run(0))
    pl.when(r >= count // 2)(lambda: run(1))


def gamma_step(table, turn, start, parts, blocks, adds, kinds, final=False):
    order, core, base, column = table
    wide = len(blocks) == 2
    rows, size = blocks[0].shape[0] // 2, blocks[0].shape[1]
    width = base.shape[1]
    block = rows // 2
    full = lambda array: pl.BlockSpec(array.shape, lambda r, order, core: (0, 0))
    row_block = pl.BlockSpec((block, width), lambda r, order, core: (r, 0))
    args = [base, column, *parts]
    specs = [full(array) for array in args]
    for _ in range(len(blocks) // 2):
        specs += [
            pl.BlockSpec((block, size), lambda r, order, core: (jnp.minimum(r, 3), 0)),
            pl.BlockSpec((block, size), lambda r, order, core: (jnp.maximum(r - 4, 0), 0)),
        ]
    args += [*blocks, *adds]
    specs += [row_block] * len(adds)
    if final:
        step = width // LANES
        out_shape = [jax.ShapeDtypeStruct((4 * rows * step, LANES), F32)]
        out_specs = [
            pl.BlockSpec((block * step, LANES), lambda r, order, core: (order[r // 2] * 2 + r % 2, 0))
        ]
    else:
        out_shape = [jax.ShapeDtypeStruct((4 * rows, width), kind) for kind in kinds]
        out_specs = [row_block] * len(kinds)
    return pl.pallas_call(
        functools.partial(gamma_kernel, len(parts), turn, start, wide, len(adds), final),
        grid_spec=pltpu.PrefetchScalarGridSpec(
            num_scalar_prefetch=2,
            grid=(8,),
            in_specs=specs,
            out_specs=out_specs,
            scratch_shapes=[pltpu.VMEM((2, size, width), BF16)],
        ),
        out_shape=out_shape,
        compiler_params=pltpu.CompilerParams(vmem_limit_bytes=32 << 20),
        cost_estimate=pl.CostEstimate(
            flops=16 * rows * size * width,
            bytes_accessed=16 * rows * size + 4 * len(parts) * size * width + 32 * rows * width,
            transcendentals=0,
        ),
    )(order, core, *args)


def shifted(part, axis, n):
    return [part] + [lax.ppermute(part, axis, [(k, (k + d) % n) for k in range(n)]) for d in range(1, n)]


def local_four(integrals, occ_energy, vir_energy, round_owner):
    n_aux = lax.axis_size("aux")
    me = lax.axis_index("occ").astype(jnp.int32)
    core = lax.axis_index("vir").astype(jnp.int32)
    by_orbital = lax.optimization_barrier(jnp.transpose(integrals[0], (1, 0, 2)))
    rows, width = by_orbital.shape[1:]
    is_mid = (me == 1) | (me == 2)
    odd = me % 2
    orbital = lambda k: lax.dynamic_index_in_dim(by_orbital, k, 0, keepdims=False)

    own = [orbital(round_owner[t]) for t in range(ROUNDS)]
    across = orbital(me ^ 3)
    beside = lax.ppermute(jnp.concatenate([own[0], orbital(me ^ 1)], axis=0), "occ", PAIRS)
    b3_mid = lax.ppermute(across, "occ", MIDDLE)
    b2 = lax.ppermute(orbital(me ^ 2), "occ", SKIPS)
    b3_end = lax.ppermute(across, "occ", ENDS)
    near = [(beside, 0), (lax.ppermute(own[1], "occ", PAIRS), 0)]

    energy_i = lax.dynamic_slice_in_dim(occ_energy, me, 1)
    energy_j = jnp.take(occ_energy, round_owner)
    bases = [
        energy_i + energy_j[:, None] - lax.dynamic_slice_in_dim(vir_energy, k * width, width)[None, :]
        for k in (core, 1 - core)
    ]
    order = jnp.arange(4, dtype=jnp.int32) ^ (me & 2)
    table = (order, core[None], jnp.concatenate(bases, axis=0), vir_energy[:, None])

    chunks = column_chunks(width)
    count = len(chunks)
    wide = count - NARROW
    half, mid, part, got, total = [None] * count, [None] * count, [None] * count, [None] * count, []

    for t in range(ROUNDS):
        members = [c for c in range(count) if chunks[c][0] == t]
        packed = pack(odd[None], own[t], near[t], [chunks[c][1:] for c in members])
        for c, array in zip(members, packed):
            half[c] = array

    def hop(c, *done):
        mid[c] = lax.ppermute(after(half[c], *done), "occ", MIDDLE)

    hop(0, b3_mid)
    hop(1, b2)
    none = jnp.zeros((1,), jnp.int32)
    (mine_near,) = pack(none, orbital(me), (beside, 1), [(0, width)])
    (mine_far,) = pack(none, b2, (jnp.where(is_mid, b3_mid, b3_end), 0), [(0, width)])
    mine_far = after(mine_far, mid[0], near[1][0])
    mine_near_swap = lax.ppermute(mine_near, "vir", SWAP)
    mine_far_swap = lax.ppermute(mine_far, "vir", SWAP)
    pending = []

    def settle(acc, there, *done):
        c, turn, start, parts, blocks = pending.pop(0)
        parts = [after(parts[0], *done), *parts[1:]] if done else parts
        if c >= wide:
            last = c == count - 1
            adds = [*acc, there] if last else acc
            return gamma_step(table, turn, start, parts, blocks, adds, (F32,), final=last), there
        kinds = (F32, F32 if c < wide - 1 else SEND)
        acc = gamma_step(table, turn, start, parts, blocks, acc, kinds)
        if c == wide - 1:
            there = lax.ppermute(acc[1], "vir", SWAP)
            acc = acc[:1]
        return acc, there

    acc, there = (), None
    for c, (turn, start, size) in enumerate(chunks):
        if c + 2 < count:
            hop(c + 2, mid[c], mine_near_swap, *([mine_far_swap] if c else []))
        end = lax.ppermute(mid[c], "occ", OUTWARD)
        if c + 1 < count:
            end = after(end, mid[c + 1])
        here = mid[c]
        if c == 0:
            here = after(here, near[1][0], mine_near_swap, mine_far_swap)
        if c > 1:
            here = after(here, *total[c - 2])
        if c:
            here = after(here, part[c - 1])
        far = jnp.where(is_mid, here, end)
        blocks = [half[c], far]
        if c < wide:
            part[c] = pair_sum(odd[None], *blocks, [mine_near, mine_far, mine_near_swap, mine_far_swap])
        else:
            blocks += [lax.ppermute(half[c], "vir", SWAP), lax.ppermute(far, "vir", SWAP)]
            part[c] = jnp.concatenate(
                [pair_sum(odd[None], *blocks[2 * h : 2 * h + 2], [mine_near, mine_far]) for h in range(2)], axis=0
            )
        got[c] = shifted(part[c], "aux", n_aux)
        pending.append((c, turn, start, got[c], blocks))
        if c:
            acc, there = settle(acc, there, part[c])
            total.append(acc)
    acc, there = settle(acc, there)
    return acc[0].reshape(4, rows, 1, width)


def local_any(integrals, occ_energy, vir_energy, round_owner):
    n_aux = lax.axis_size("aux")
    me = lax.axis_index("occ")
    core = lax.axis_index("vir")
    x = integrals[0]
    rows, n_occ, width = x.shape
    mine = lax.all_to_all(x, "occ", split_axis=1, concat_axis=0, tiled=True)[:, 0]
    energy_i = lax.dynamic_slice_in_dim(occ_energy, me, 1)
    energy_a = lax.dynamic_slice_in_dim(vir_energy, core * width, width)
    gamma = jnp.zeros(mine.shape, F32)
    for turn in range(ROUNDS):
        owner = round_owner[turn]
        own = lax.dynamic_index_in_dim(x, owner, 1, keepdims=False)
        whole = lax.all_gather(own, "occ", axis=0, tiled=True)
        other = lax.ppermute(whole, "vir", SWAP)
        energy_j = lax.dynamic_slice_in_dim(occ_energy, owner, 1)
        base = (energy_i + energy_j - energy_a)[None, :]
        for which, block in ((core, whole), (1 - core, other)):
            energy_b = lax.dynamic_slice_in_dim(vir_energy, which * width, width)[:, None]
            part = jnp.einsum("pb,pa->ba", block, mine, preferred_element_type=F32).astype(BF16)
            pair = sum(p.astype(F32) for p in shifted(part, "aux", n_aux))
            amplitude = (pair / (base - energy_b)).astype(BF16)
            gamma = gamma + jnp.dot(block, amplitude, preferred_element_type=F32)
    return gamma.reshape(-1, rows, 1, width)


def solution(mesh):
    placed = (P("occ", "aux", "grp", "vir"), P("grp"), P("grp"), P("grp"))
    local = local_four if mesh.shape["occ"] == 4 else local_any
    return jax.shard_map(
        local, mesh=mesh, in_specs=placed, out_specs=P("grp", "aux", "occ", "vir"), check_vma=False
    )
```
